32 devices in a mesh: seq: 16 (over z, y, core), fsdp: 2 (over x).
Axes of the slice: x: 2, y: 2, z: 4, core: 2. Of those that a mesh axis runs over, the one named last changes fastest.
Arguments:
- queries: bfloat16 [2, 2048, 2560], P('fsdp', 'seq'), may hold values from -8 to 8
- key_value_sets: bfloat16 [2, 4, 2048, 2560], P('fsdp', None, 'seq'), may hold values from -8 to 8
- cache_offsets: int32 [16], replicated, may hold values from 0 to 1
- cache_lengths: int32 [2, 16], P('fsdp'), may hold values from 1 to 128, as said below
- out_weight: bfloat16 [2560, 5120], P(('seq', 'fsdp')), may hold values from -0.125 to 0.125
- residual: bfloat16 [2, 2048, 5120], P('fsdp', 'seq'), may hold values from -2.5 to 2.5
- gate_scale: float32 [2, 5120], P('fsdp'), may hold values from 0.5 to 1.5
Outputs:
- updated: bfloat16 [2, 2048, 5120], P('fsdp', 'seq')
The draws below stay inside these ranges and needn't reach their ends.
Inputs may be any that keep to these rules, and one draw needn't show every extreme that they name: `cache_lengths`: in every video some tile holds all 128 cached tokens.
All inputs are finite; a program needn't handle non-finite values.
Results may differ from the reference program's by a relative error of at most 0.0053.
Values may be sent and summed in bfloat16 or wider, within the bound.
A program may use at most 192 MiB of HBM per device.

```python
import math
import jax
import jax.numpy as jnp
from jax import lax

D = 5120
HDIM = 128
HEADS = 20
TILE = 128
INNER = 2560
NTILES = 16
TOKENS = 2048
VIDEOS = 2


def rough(key, shape):
    return jnp.clip(1.5 * jax.random.normal(key, shape, jnp.float32), -6.0, 6.0)


def draw_queries(key, part):
    field = rough(jax.random.fold_in(key, 1), (VIDEOS, NTILES, TILE, HEADS * HDIM))
    return field.reshape(VIDEOS, TOKENS, HEADS * HDIM).astype(jnp.bfloat16)


def draw_key_value_sets(key, part):
    field = rough(jax.random.fold_in(key, 2), (VIDEOS, 4, NTILES, TILE, HEADS * HDIM))
    return field.reshape(VIDEOS, 4, TOKENS, HEADS * HDIM).astype(jnp.bfloat16)


def draw_cache_lengths(key, part):
    length_key, full_key = jax.random.split(jax.random.fold_in(key, 3))
    counts = jax.random.randint(length_key, (VIDEOS, NTILES), 1, TILE + 1)
    full_tile = jax.random.randint(full_key, (VIDEOS, 1), 0, NTILES)
    tile_ids = jnp.arange(NTILES, dtype=jnp.int32)[None, :]
    return jnp.where(tile_ids == full_tile, TILE, counts).astype(jnp.int32)


def place_ends(array, key, least, top_value):
    index_at = [jax.random.randint(jax.random.fold_in(key, axis), (), 0, length) for axis, length in enumerate(array.shape)]
    main_axis = array.shape.index(max(array.shape))
    next_to = index_at[:main_axis] + [(index_at[main_axis] + 1) % array.shape[main_axis]] + index_at[main_axis + 1:]
    return array.at[tuple(index_at)].set(least).at[tuple(next_to)].set(top_value)


def block_levels(own_key, extent, cuts, least, largest):
    gain, own = 1.0, jax.random.fold_in(own_key, 6)
    for position, shards_of in cuts:
        draws = jnp.exp(jax.random.uniform(jax.random.fold_in(own, position), (shards_of,), jnp.float32, least / len(cuts), largest / len(cuts)))
        gain = gain * jnp.repeat(draws, extent[position] // shards_of).reshape([-1 if axis == position else 1 for axis in range(len(extent))])
    return gain


def noise(own_key, dims, width, bound, cuts=(), held_as=jnp.bfloat16):
    level = block_levels(own_key, dims, cuts, -0.22, 0.18) if cuts else 1.0
    entries = jax.random.normal(own_key, dims, jnp.float32) * width * level
    return jnp.minimum(jnp.maximum(entries, -bound), bound).astype(held_as)


def setup_inputs(seed: int = 0) -> dict:
    key_list = jax.random.split(jax.random.key(seed), 8)
    queries = draw_queries(jax.random.fold_in(key_list[7], 71), 0)
    key_value_sets = draw_key_value_sets(jax.random.fold_in(key_list[7], 71), 0)
    cache_offsets = place_ends(jax.random.randint(key_list[2], (NTILES,), 0, 2), jax.random.fold_in(key_list[2], 1), 0, 1).astype(jnp.int32)
    cache_lengths = draw_cache_lengths(jax.random.fold_in(key_list[7], 71), 0)
    out_weight = noise(key_list[4], (INNER, D), INNER ** -0.5, 0.125, ((0, 32),))
    residual = noise(key_list[5], (VIDEOS, TOKENS, D), 0.3, 2.5, ((0, 2), (1, 16)))
    gate_scale = jnp.clip(0.5 + 1.0 * jax.random.uniform(key_list[6], (VIDEOS, D), jnp.float32) ** block_levels(key_list[6], (VIDEOS, D), ((0, 2),), -0.2, 0.2), 0.5, 1.5)
    return dict(queries=queries, key_value_sets=key_value_sets, cache_offsets=cache_offsets, cache_lengths=cache_lengths, out_weight=out_weight, residual=residual, gate_scale=gate_scale)


def window_valid(tile_index, offset, padded_lengths, tile_count):
    span_tiles = tile_index - 1 + jnp.arange(3, dtype=jnp.int32)
    span_allowed = jnp.repeat((span_tiles >= 0) & (span_tiles < tile_count), TILE)
    first_cache = (tile_index - 1 + offset).astype(jnp.int32)
    cache_counts = lax.dynamic_slice_in_dim(padded_lengths, first_cache + 1, 2)
    positions = jnp.arange(TILE, dtype=jnp.int32)
    cache_allowed = (positions[None, :] < cache_counts[:, None]).reshape(2 * TILE)
    return jnp.concatenate([span_allowed, cache_allowed])

def attend(tile_queries, keyset, valueset, allowed):
    score_scale = 1.0 / math.sqrt(HDIM)
    query_heads = tile_queries.astype(jnp.float32).reshape(TILE, HEADS, HDIM)
    key_heads = keyset.astype(jnp.float32).reshape(5 * TILE, HEADS, HDIM)
    value_heads = valueset.astype(jnp.float32).reshape(5 * TILE, HEADS, HDIM)
    scores = jnp.einsum('qhd,khd->hqk', query_heads, key_heads) * score_scale
    scores = jnp.where(allowed[None, None, :], scores, -1e+30)
    row_peak = lax.optimization_barrier(jnp.max(scores, axis=-1, keepdims=True))
    expont = jnp.exp(scores - row_peak)
    probs = (expont / lax.optimization_barrier(jnp.sum(expont, axis=-1, keepdims=True))).astype(jnp.bfloat16)
    attended = jnp.einsum('hqk,khd->qhd', probs.astype(jnp.float32), value_heads)
    return attended.reshape(TILE, HEADS * HDIM).astype(jnp.bfloat16)

def reference(queries, key_value_sets, cache_offsets, cache_lengths, out_weight, residual, gate_scale):
    inner_width = HEADS * HDIM

    def one_video(video_index):
        video_queries = queries[video_index].reshape(NTILES, TILE, inner_width)
        padded = jnp.pad(key_value_sets[video_index], ((0, 0), (TILE, TILE), (0, 0)))
        padded_lengths = jnp.pad(cache_lengths[video_index], 1)

        def one_tile(tile_index):
            span_part = lax.dynamic_slice_in_dim(padded[0:2], (tile_index * TILE).astype(jnp.int32), 3 * TILE, 1)
            offset = cache_offsets[tile_index]
            cached = lax.dynamic_slice_in_dim(padded[2:4], ((tile_index + offset) * TILE).astype(jnp.int32), 2 * TILE, 1)
            allowed = window_valid(tile_index, offset, padded_lengths, NTILES)
            keyset = jnp.concatenate([span_part[0], cached[0]], 0)
            valueset = jnp.concatenate([span_part[1], cached[1]], 0)
            return attend(video_queries[tile_index], keyset, valueset, allowed)
        attended = lax.map(one_tile, jnp.arange(NTILES, dtype=jnp.int32)).reshape(TOKENS, inner_width)
        projected = jnp.dot(attended, out_weight, preferred_element_type=jnp.float32)
        return (residual[video_index].astype(jnp.float32) + gate_scale[video_index][None, :] * projected).astype(jnp.bfloat16)
    return lax.map(one_video, jnp.arange(VIDEOS, dtype=jnp.int32))
```

```python
import functools
import math

import jax
import jax.numpy as jnp
from jax import lax
from jax.experimental import pallas as pl
from jax.experimental.pallas import tpu as pltpu
from jax.sharding import PartitionSpec as P

HDIM = 128
HEADS = 20
TILE = 128
NEG = -1e30
SCALE = 1.0 / math.sqrt(HDIM)
SCALE2 = SCALE / math.log(2.0)
MESH = pl.DeviceIdType.MESH


def extended(cells, sides, width):
    for axis, dim in sides:
        count = lax.axis_size(axis)
        ends = count - 1
        head = lax.slice_in_dim(cells, 0, width, axis=dim)
        tail = lax.slice_in_dim(cells, cells.shape[dim] - width, cells.shape[dim], axis=dim)
        cells = jnp.concatenate(
            [
                lax.ppermute(tail, axis, [(i, (i + 1) % count) for i in range(ends)]),
                cells,
                lax.ppermute(head, axis, [((i + 1) % count, i) for i in range(ends)]),
            ],
            axis=dim,
        )
    return cells


def window_valid(tile_index, offset, padded_lengths, tile_count):
    span_tiles = tile_index - 1 + jnp.arange(3, dtype=jnp.int32)
    span_allowed = jnp.repeat((span_tiles >= 0) & (span_tiles < tile_count), TILE)
    first_cache = tile_index - 1 + offset
    cache_counts = lax.dynamic_slice_in_dim(padded_lengths, first_cache + 1, 2)
    positions = jnp.arange(TILE, dtype=jnp.int32)
    cache_allowed = (positions[None, :] < cache_counts[:, None]).reshape(2 * TILE)
    return jnp.concatenate([span_allowed, cache_allowed])


def attend(tile_queries, keyset, valueset, allowed):
    query_heads = tile_queries.reshape(TILE, HEADS, HDIM)
    key_heads = keyset.reshape(5 * TILE, HEADS, HDIM)
    value_heads = valueset.reshape(5 * TILE, HEADS, HDIM)
    scores = (
        jnp.einsum("qhd,khd->hqk", query_heads, key_heads, preferred_element_type=jnp.float32)
        * SCALE
    )
    scores = jnp.where(allowed[None, None, :], scores, NEG)
    row_peak = jnp.max(scores, axis=-1, keepdims=True)
    expont = jnp.exp(scores - row_peak)
    probs = (expont / jnp.sum(expont, axis=-1, keepdims=True)).astype(jnp.bfloat16)
    attended = jnp.einsum("hqk,khd->qhd", probs, value_heads, preferred_element_type=jnp.float32)
    return attended.reshape(TILE, HEADS * HDIM).astype(jnp.bfloat16)


def plain(queries, key_value_sets, cache_offsets, cache_lengths, out_weight, residual, gate_scale):
    tile_count = cache_lengths.shape[1]
    tiles_here = queries.shape[1] // TILE
    device = lax.axis_index("seq")
    padded = extended(key_value_sets, (("seq", 2),), TILE)[0]
    padded_lengths = jnp.pad(cache_lengths[0], 1)

    def one_tile(local_tile):
        tile_index = device * tiles_here + local_tile
        span_part = padded[0:2]
        offset = cache_offsets[tile_index]
        cached = lax.dynamic_slice_in_dim(padded[2:4], (local_tile + offset) * TILE, 2 * TILE, 1)
        allowed = window_valid(tile_index, offset, padded_lengths, tile_count)
        tile_queries = queries[0]
        keyset = jnp.concatenate([span_part[0], cached[0]], 0)
        valueset = jnp.concatenate([span_part[1], cached[1]], 0)
        return attend(tile_queries, keyset, valueset, allowed)

    attended = jax.vmap(one_tile)(jnp.arange(tiles_here, dtype=jnp.int32)).reshape(
        tiles_here * TILE, queries.shape[2]
    )
    whole_weight = lax.all_gather(out_weight, ("seq", "fsdp"), axis=0, tiled=True)
    projected = jnp.dot(attended, whole_weight, preferred_element_type=jnp.float32)
    result = residual[0].astype(jnp.float32) + gate_scale[0][None, :] * projected
    return result.astype(jnp.bfloat16)[None]


def order(groups, stages, depth):
    steps = [("P", k, 0) for k in range(stages)]
    steps += [("T", g, 0) for g in range(groups)]
    steps += [("M", 0, 0)]
    for i in range(max(groups, stages)):
        if i < stages and depth > 2:
            steps.append(("R", i, 1))
        if 1 <= i < groups:
            steps.append(("M", i, 0))
    steps += [("F", g, 0) for g in range(groups)]
    return steps + [("R", k, hop) for hop in range(2, depth - 1) for k in range(stages)]


def kernel(
    n, groups, stages,
    off_ref, len_ref, q_hbm, kv_hbm, w_hbm, out_ref,
    qall, kv, bias, own_o, own_s, osend, ssend, orecv, srecv, abuf, wbuf, csend,
    load_sem, own_w_sem, own_c_sem,
    q_ss, q_rs, o_ss, o_rs, t_ss, t_rs, a_ss, a_rs, w_ss, w_rs, z_ss, z_rs, p_ss, p_rs, c_ss, c_rs,
    d_ss, d_rs,
):
    s = lax.axis_index("seq")
    x = lax.axis_index("fsdp")
    core = s % 2
    y = (s // 2) % 2
    z = s // 4
    depth = n // 4
    rows = w_hbm.shape[0]
    width = w_hbm.shape[1] // 4
    piece = width // stages
    per = HEADS // groups
    span = per * HDIM
    me = y * 2 + x
    has_left, has_right = s > 0, s < n - 1
    has_down, has_up = z > 0, z < depth - 1

    def at(seq, fsdp):
        return {"seq": seq, "fsdp": fsdp}

    left, right = at(s - 1, x), at(s + 1, x)
    down, up = at(s - 4, x), at(s + 4, x)
    partner = at(s + 1 - 2 * core, x)
    s_y = s + 2 - 4 * y
    peers = (
        (at(s, 1 - x), y * 2 + 1 - x),
        (at(s_y, x), (1 - y) * 2 + x),
        (at(s_y, 1 - x), (1 - y) * 2 + 1 - x),
    )
    sides = ((has_left, left), (has_right, right))
    thin_out = ((z == depth - 2) & (y == 1), (z == 1) & (y == 0))
    thin_in = ((z == depth - 1) & (y == 1), (z == 0) & (y == 0))
    gives_up, gives_down = (z == depth - 2) & (y == 0), (z == 1) & (y == 1)
    gives = gives_up | gives_down
    takes = thin_in[0] | thin_in[1]
    over = jnp.where(gives_up, s + 6, s - 6)
    under = jnp.where(thin_in[0], s - 6, s + 6)
    across = (x, 1 - x)

    def remote(src, dst, ss, rs, to):
        return pltpu.make_async_remote_copy(
            src_ref=src, dst_ref=dst, send_sem=ss, recv_sem=rs, device_id=to, device_id_type=MESH
        )

    load_q = pltpu.make_async_copy(q_hbm.at[0], qall.at[pl.ds(TILE, TILE)], load_sem.at[0])
    load_kv = pltpu.make_async_copy(kv_hbm.at[0], kv, load_sem.at[1])
    load_kv.start()
    load_q.start()

    barrier = pltpu.get_barrier_semaphore()
    for to, _ in peers:
        pl.semaphore_signal(barrier, inc=1, device_id=to, device_id_type=MESH)
    for there, to in sides + ((has_down, down), (has_up, up)):
        @pl.when(there)
        def _(to=to):
            pl.semaphore_signal(barrier, inc=1, device_id=to, device_id_type=MESH)
    for there, seq in ((gives, over), (takes, under)):
        @pl.when(there)
        def _(seq=seq):
            for fsdp in across:
                pl.semaphore_signal(
                    barrier, inc=1, device_id=at(seq, fsdp), device_id_type=MESH
                )
    met = [there.astype(jnp.int32) for there in (has_left, has_right, has_down, has_up)]
    met += [2 * there.astype(jnp.int32) for there in (gives, takes)]
    pl.semaphore_wait(barrier, 3 + sum(met))

    def cols(g):
        return pl.ds(pl.multiple_of(g * span, span), span)

    def q_copy(side, g):
        to = sides[side][1]
        dst = qall.at[pl.ds((1 - side) * 2 * TILE, TILE), cols(g)]
        return remote(q_hbm.at[0, :, cols(g)], dst, q_ss.at[side, g], q_rs.at[1 - side, g], to)

    def q_arrival(side, g):
        dst = qall.at[pl.ds(side * 2 * TILE, TILE), cols(g)]
        return remote(dst, dst, q_ss.at[side, g], q_rs.at[side, g], sides[side][1])

    def o_copy(side, g):
        to = sides[side][1]
        return remote(
            osend.at[side, cols(g)], orecv.at[1 - side, cols(g)],
            o_ss.at[side, g], o_rs.at[1 - side, g], to,
        )

    def o_arrival(side, g):
        dst = orecv.at[side, cols(g)]
        return remote(dst, dst, o_ss.at[side, g], o_rs.at[side, g], sides[side][1])

    def t_copy(side, g):
        to = sides[side][1]
        return remote(
            ssend.at[side, g], srecv.at[1 - side, g], t_ss.at[side, g], t_rs.at[1 - side, g], to
        )

    def t_arrival(side, g):
        dst = srecv.at[side, g]
        return remote(dst, dst, t_ss.at[side, g], t_rs.at[side, g], sides[side][1])

    def a_copy(kind, g):
        slot = peers[1][1] if kind == 2 else me
        block = abuf.at[pl.ds(pl.multiple_of(slot * TILE, TILE), TILE), cols(g)]
        to = peers[kind % 2][0]
        return remote(block, block, a_ss.at[kind, g], a_rs.at[kind, g], to)

    def a_arrival(kind, g):
        theirs = abuf.at[pl.ds(pl.multiple_of(peers[kind][1] * TILE, TILE), TILE), cols(g)]
        return remote(theirs, theirs, a_ss.at[kind, g], a_rs.at[kind, g], peers[kind][0])

    def w_piece(slot, k):
        return w_hbm.at[:, pl.ds(pl.multiple_of(slot * width + k * piece, piece), piece)]

    def w_slot(k, y_of, x_of):
        return wbuf.at[k, z, y_of, core, pl.ds(pl.multiple_of(x_of * rows, rows), rows)]

    def w_own(k):
        return pltpu.make_async_copy(w_piece(me, k), w_slot(k, y, x), own_w_sem.at[k])

    def w_copy(kind, k):
        to, slot = peers[kind]
        return remote(w_piece(slot, k), w_slot(k, y, x), w_ss.at[kind, k], w_rs.at[kind, k], to)

    def w_arrival(kind, k):
        to, slot = peers[kind]
        dst = w_slot(k, slot // 2, slot % 2)
        return remote(dst, dst, w_ss.at[kind, k], w_rs.at[kind, k], to)

    def d_copy(kind, k):
        slot = (1 - y) * 2 + across[kind]
        return remote(
            w_piece(slot, k), w_slot(k, y, x), d_ss.at[kind, k], d_rs.at[kind, k],
            at(over, across[kind]),
        )

    def d_arrival(kind, k):
        plane = jnp.where(thin_in[0], z - 1, z + 1)
        dst = wbuf.at[
            k, plane, 1 - y, core, pl.ds(pl.multiple_of(across[kind] * rows, rows), rows)
        ]
        return remote(dst, dst, d_ss.at[kind, k], d_rs.at[kind, k], at(under, across[kind]))

    def z_block(way, hop, k, thin):
        plane = z - hop if way == 0 else z + hop
        return wbuf.at[k, plane, 1 - way, core] if thin else wbuf.at[k, plane, :, core]

    def z_copy(way, hop, k, thin):
        block = z_block(way, hop, k, thin)
        return remote(
            block, block, z_ss.at[way, hop, k], z_rs.at[way, hop, k], up if way == 0 else down
        )

    def z_arrival(way, hop, k, thin):
        block = z_block(way, hop, k, thin)
        return remote(
            block, block, z_ss.at[way, hop - 1, k], z_rs.at[way, hop - 1, k],
            down if way == 0 else up,
        )

    def z_out(way, hop, k, act):
        if hop > 0:
            act(z_copy(way, hop, k, False))
            return
        for thin, there in ((True, thin_out[way]), (False, jnp.logical_not(thin_out[way]))):
            @pl.when(there)
            def _(thin=thin):
                act(z_copy(way, hop, k, thin))

    def z_in(way, hop, k):
        if hop > 1:
            z_arrival(way, hop, k, False).wait_recv()
            return

        @pl.when(thin_in[way])
        def _():
            z_arrival(way, hop, k, True).wait_recv()
            for kind in range(2):
                d_arrival(kind, k).wait_recv()

        @pl.when(jnp.logical_not(thin_in[way]))
        def _():
            z_arrival(way, hop, k, False).wait_recv()

    def p_copy(plane, k):
        block = wbuf.at[k, plane, :, core]
        return remote(block, block, p_ss.at[plane, k], p_rs.at[plane, k], partner)

    def p_arrival(plane, k):
        block = wbuf.at[k, plane, :, 1 - core]
        return remote(block, block, p_ss.at[plane, k], p_rs.at[plane, k], partner)

    def c_place(slot, k):
        return out_ref.at[:, pl.ds(pl.multiple_of(slot * width + k * piece, piece), piece)]

    def c_rows(slot, k):
        return csend.at[k, pl.ds(pl.multiple_of(slot * TILE, TILE), TILE)]

    def c_own(k):
        return pltpu.make_async_copy(c_rows(me, k), c_place(me, k), own_c_sem.at[k])

    def c_copy(kind, k):
        to, slot = peers[kind]
        return remote(c_rows(slot, k), c_place(me, k), c_ss.at[kind, k], c_rs.at[kind, k], to)

    def c_arrival(kind, k):
        to, slot = peers[kind]
        dst = c_place(slot, k)
        return remote(dst, dst, c_ss.at[kind, k], c_rs.at[kind, k], to)

    def each(count, body):
        lax.fori_loop(0, count, lambda i, c: (body(i), c)[1], jnp.int32(0))

    def on_sides(body):
        for side, (there, _) in enumerate(sides):
            @pl.when(there)
            def _(side=side):
                body(side)

    def relay(hop, k):
        for way, (there, onward) in enumerate(
            ((z >= hop, has_up), (z + hop < depth, has_down))
        ):
            @pl.when(there)
            def _(way=way, onward=onward):
                z_in(way, hop, k)
                if hop < depth - 1:
                    @pl.when(onward)
                    def _():
                        z_out(way, hop, k, lambda copy: copy.start())
                p_copy(z - hop if way == 0 else z + hop, k).start()

    def begin_w(k):
        w_own(k).start()
        for kind in range(3):
            w_copy(kind, k).start()

        @pl.when(gives)
        def _():
            for kind in range(2):
                d_copy(kind, k).start()

    for step in range(max(groups, stages)):
        if step < stages:
            begin_w(step)
        if step < groups:
            on_sides(lambda side: q_copy(side, step).start())

    here = len_ref[0, s]
    for_left = jnp.where(off_ref[jnp.maximum(s - 1, 0)] == 1, here, 0)
    for_right = jnp.where(off_ref[jnp.minimum(s + 1, n - 1)] == 0, here, 0)
    lane = lax.broadcasted_iota(jnp.int32, (TILE, 3 * TILE), 1)
    row = lax.broadcasted_iota(jnp.int32, (TILE, 3 * TILE), 0)
    limit = jnp.where(lane < TILE, for_left, jnp.where(lane < 2 * TILE, here, for_right))
    bias[...] = jnp.where(row < limit, 0.0, NEG)

    for side, (there, _) in enumerate(sides):
        @pl.when(jnp.logical_not(there))
        def _(side=side):
            qall[pl.ds(side * 2 * TILE, TILE), :] = jnp.zeros((TILE, HEADS * HDIM), jnp.bfloat16)
            orecv[side] = jnp.zeros((HEADS * HDIM, TILE), jnp.bfloat16)
            srecv[side] = jnp.full((groups, 8, TILE), NEG, jnp.float32)

    def plane_step(k):
        w_own(k).wait()
        for kind in range(3):
            w_arrival(kind, k).wait_recv()
        for way, there in enumerate((has_up, has_down)):
            @pl.when(there)
            def _(way=way):
                z_out(way, 0, k, lambda copy: copy.start())
        p_copy(z, k).start()

    load_q.wait()
    load_kv.wait()

    def attend_group(g):
        on_sides(lambda side: q_arrival(side, g).wait_recv())

        def head(i):
            at_head = pl.ds(pl.multiple_of((g * per + i) * HDIM, HDIM), HDIM)
            keys = jnp.concatenate([kv[0, :, at_head], kv[2, :, at_head]], 0)
            values = jnp.concatenate([kv[1, :, at_head], kv[3, :, at_head]], 0)
            asked = qall[:, at_head]
            scores = lax.dot_general(
                keys, asked, (((1,), (1,)), ((), ())), preferred_element_type=jnp.float32
            )
            near = scores[:TILE]
            far = scores[TILE:] + bias[...]
            peak = jnp.maximum(
                jnp.max(near, axis=0, keepdims=True), jnp.max(far, axis=0, keepdims=True)
            )
            near = jnp.exp2((near - peak) * SCALE2)
            far = jnp.exp2((far - peak) * SCALE2)
            total = jnp.sum(near, axis=0, keepdims=True) + jnp.sum(far, axis=0, keepdims=True)
            weights = jnp.concatenate([near, far], 0).astype(jnp.bfloat16)
            mixed = lax.dot_general(
                values, weights, (((0,), (0,)), ((), ())), preferred_element_type=jnp.float32
            )
            mixed = mixed * (1.0 / total)
            level = peak * SCALE + jnp.log(total)
            osend[0, at_head, :] = mixed[:, :TILE].astype(jnp.bfloat16)
            own_o[at_head, :] = mixed[:, TILE : 2 * TILE]
            osend[1, at_head, :] = mixed[:, 2 * TILE :].astype(jnp.bfloat16)
            ssend[0, g, pl.ds(i, 1), :] = level[:, :TILE]
            own_s[g, pl.ds(i, 1), :] = level[:, TILE : 2 * TILE]
            ssend[1, g, pl.ds(i, 1), :] = level[:, 2 * TILE :]

        for i in range(per):
            head(i)

        def give(side):
            t_copy(side, g).start()
            o_copy(side, g).start()

        on_sides(give)

    def merge_group(g):
        def arrive(side):
            t_arrival(side, g).wait_recv()
            o_arrival(side, g).wait_recv()

        on_sides(arrive)

        def head(i):
            at_head = pl.ds(pl.multiple_of((g * per + i) * HDIM, HDIM), HDIM)
            l0 = own_s[g, pl.ds(i, 1), :]
            l1 = srecv[0, g, pl.ds(i, 1), :]
            l2 = srecv[1, g, pl.ds(i, 1), :]
            top = jnp.maximum(l0, jnp.maximum(l1, l2))
            e0, e1, e2 = jnp.exp(l0 - top), jnp.exp(l1 - top), jnp.exp(l2 - top)
            both = e0 + e1 + e2
            part = 1.0 / both
            total = (
                own_o[at_head, :] * (e0 * part)
                + orecv[0, at_head, :].astype(jnp.float32) * (e1 * part)
                + orecv[1, at_head, :].astype(jnp.float32) * (e2 * part)
            )
            mine = pl.ds(pl.multiple_of(me * TILE, TILE), TILE)
            abuf[mine, at_head] = jnp.transpose(total.astype(jnp.bfloat16))

        for i in range(per):
            head(i)
        a_copy(1, g).start()
        a_copy(0, g).start()

    def forward(g):
        a_arrival(1, g).wait_recv()
        a_copy(2, g).start()

    acts = {"P": plane_step, "T": attend_group, "M": merge_group, "F": forward}
    for act, which, hop in order(groups, stages, depth):
        if act == "R":
            relay(hop, which)
        else:
            acts[act](which)

    def a_wait(g):
        a_arrival(0, g).wait_recv()
        a_arrival(2, g).wait_recv()

    each(groups, a_wait)

    def stage(k):
        if depth > 1:
            relay(depth - 1, k)
        for plane in range(depth):
            p_arrival(plane, k).wait_recv()
        block = wbuf[k].reshape(n * 2 * rows, piece)
        product = jnp.dot(abuf[...], block, preferred_element_type=jnp.float32)
        csend[k] = product.astype(jnp.bfloat16)
        for kind in range(3):
            c_copy(kind, k).start()
        c_own(k).start()

    each(stages, stage)

    def finish_stage(k):
        c_own(k).wait()
        for kind in range(3):
            c_arrival(kind, k).wait_recv()
            c_copy(kind, k).wait_send()
            w_copy(kind, k).wait_send()

        @pl.when(gives)
        def _():
            for kind in range(2):
                d_copy(kind, k).wait_send()

        for plane in range(depth):
            p_copy(plane, k).wait_send()
        for hop in range(depth - 1):
            for way, there in enumerate(
                (has_up & (z >= hop), has_down & (z + hop < depth))
            ):
                @pl.when(there)
                def _(way=way, hop=hop):
                    z_out(way, hop, k, lambda copy: copy.wait_send())

    def finish_group(g):
        for kind in range(3):
            a_copy(kind, g).wait_send()

        def sent(side):
            q_copy(side, g).wait_send()
            o_copy(side, g).wait_send()
            t_copy(side, g).wait_send()

        on_sides(sent)

    each(groups, finish_group)
    each(stages, finish_stage)


GROUPS = 4
PIECE = 256


def fused(queries, key_value_sets, cache_offsets, cache_lengths, out_weight, residual, gate_scale):
    n = lax.axis_size("seq")
    inner = queries.shape[2]
    rows, model = out_weight.shape
    depth = n // 4
    stages = model // 4 // PIECE
    bf16, f32 = jnp.bfloat16, jnp.float32
    dma = pltpu.SemaphoreType.DMA
    smem = pl.BlockSpec(memory_space=pltpu.SMEM)
    hbm = pl.BlockSpec(memory_space=pltpu.HBM)
    projected = pl.pallas_call(
        functools.partial(kernel, n, GROUPS, stages),
        out_shape=jax.ShapeDtypeStruct((TILE, model), bf16),
        in_specs=[smem, smem, hbm, hbm, hbm],
        out_specs=pl.BlockSpec(memory_space=pl.ANY),
        scratch_shapes=[
            pltpu.VMEM((3 * TILE, inner), bf16),
            pltpu.VMEM((4, TILE, inner), bf16),
            pltpu.VMEM((TILE, 3 * TILE), f32),
            pltpu.VMEM((inner, TILE), f32),
            pltpu.VMEM((GROUPS, 8, TILE), f32),
            pltpu.VMEM((2, inner, TILE), bf16),
            pltpu.VMEM((2, GROUPS, 8, TILE), f32),
            pltpu.VMEM((2, inner, TILE), bf16),
            pltpu.VMEM((2, GROUPS, 8, TILE), f32),
            pltpu.VMEM((4 * TILE, inner), bf16),
            pltpu.VMEM((stages, depth, 2, 2, 2 * rows, PIECE), bf16),
            pltpu.VMEM((stages, 4 * TILE, PIECE), bf16),
            dma((2,)), dma((stages,)), dma((stages,)),
            dma((2, GROUPS)), dma((2, GROUPS)),
            dma((2, GROUPS)), dma((2, GROUPS)),
            dma((2, GROUPS)), dma((2, GROUPS)),
            dma((3, GROUPS)), dma((3, GROUPS)),
            dma((3, stages)), dma((3, stages)),
            dma((2, depth, stages)), dma((2, depth, stages)),
            dma((depth, stages)), dma((depth, stages)),
            dma((3, stages)), dma((3, stages)),
            dma((2, stages)), dma((2, stages)),
        ],
        compiler_params=pltpu.CompilerParams(
            collective_id=0, has_side_effects=True, vmem_limit_bytes=56 * 2**20
        ),
    )(cache_offsets, cache_lengths, queries, key_value_sets, out_weight)
    result = residual[0].astype(f32) + gate_scale[0][None, :] * projected.astype(f32)
    return result.astype(bf16)[None]


def shards(queries, key_value_sets, cache_offsets, cache_lengths, out_weight, residual, gate_scale):
    args = (
        queries, key_value_sets, cache_offsets, cache_lengths, out_weight, residual, gate_scale
    )
    n, f = lax.axis_size("seq"), lax.axis_size("fsdp")
    rows, model = out_weight.shape
    suits = (
        f == 2
        and n % 4 == 0
        and n > 4
        and queries.shape[:2] == (1, TILE)
        and cache_lengths.shape[1] == n
        and rows % 16 == 0
        and model % (4 * PIECE) == 0
        and HEADS % GROUPS == 0
        and HEADS // GROUPS <= 8
    )
    return fused(*args) if suits else plain(*args)


def solution(mesh):
    placed = (
        P("fsdp", "seq", None),
        P("fsdp", None, "seq", None),
        P(),
        P("fsdp", None),
        P(("seq", "fsdp"), None),
        P("fsdp", "seq", None),
        P("fsdp", None),
    )
    return jax.shard_map(
        shards, mesh=mesh, in_specs=placed, out_specs=P("fsdp", "seq", None), check_vma=False
    )
```

```python
import functools
import math

import jax
import jax.numpy as jnp
from jax import lax
from jax.experimental import pallas as pl
from jax.experimental.pallas import tpu as pltpu
from jax.sharding import PartitionSpec as P

HDIM = 128
HEADS = 20
TILE = 128
NEG = -1e30
SCALE = 1.0 / math.sqrt(HDIM)
SCALE2 = SCALE / math.log(2.0)
MESH = pl.DeviceIdType.MESH


def extended(cells, sides, width):
    for axis, dim in sides:
        count = lax.axis_size(axis)
        ends = count - 1
        head = lax.slice_in_dim(cells, 0, width, axis=dim)
        tail = lax.slice_in_dim(cells, cells.shape[dim] - width, cells.shape[dim], axis=dim)
        cells = jnp.concatenate(
            [
                lax.ppermute(tail, axis, [(i, (i + 1) % count) for i in range(ends)]),
                cells,
                lax.ppermute(head, axis, [((i + 1) % count, i) for i in range(ends)]),
            ],
            axis=dim,
        )
    return cells


def window_valid(tile_index, offset, padded_lengths, tile_count):
    span_tiles = tile_index - 1 + jnp.arange(3, dtype=jnp.int32)
    span_allowed = jnp.repeat((span_tiles >= 0) & (span_tiles < tile_count), TILE)
    first_cache = tile_index - 1 + offset
    cache_counts = lax.dynamic_slice_in_dim(padded_lengths, first_cache + 1, 2)
    positions = jnp.arange(TILE, dtype=jnp.int32)
    cache_allowed = (positions[None, :] < cache_counts[:, None]).reshape(2 * TILE)
    return jnp.concatenate([span_allowed, cache_allowed])


def attend(tile_queries, keyset, valueset, allowed):
    query_heads = tile_queries.reshape(TILE, HEADS, HDIM)
    key_heads = keyset.reshape(5 * TILE, HEADS, HDIM)
    value_heads = valueset.reshape(5 * TILE, HEADS, HDIM)
    scores = (
        jnp.einsum("qhd,khd->hqk", query_heads, key_heads, preferred_element_type=jnp.float32)
        * SCALE
    )
    scores = jnp.where(allowed[None, None, :], scores, NEG)
    row_peak = jnp.max(scores, axis=-1, keepdims=True)
    expont = jnp.exp(scores - row_peak)
    probs = (expont / jnp.sum(expont, axis=-1, keepdims=True)).astype(jnp.bfloat16)
    attended = jnp.einsum("hqk,khd->qhd", probs, value_heads, preferred_element_type=jnp.float32)
    return attended.reshape(TILE, HEADS * HDIM).astype(jnp.bfloat16)


def plain(queries, key_value_sets, cache_offsets, cache_lengths, out_weight, residual, gate_scale):
    tile_count = cache_lengths.shape[1]
    tiles_here = queries.shape[1] // TILE
    device = lax.axis_index("seq")
    padded = extended(key_value_sets, (("seq", 2),), TILE)[0]
    padded_lengths = jnp.pad(cache_lengths[0], 1)

    def one_tile(local_tile):
        tile_index = device * tiles_here + local_tile
        span_part = padded[0:2]
        offset = cache_offsets[tile_index]
        cached = lax.dynamic_slice_in_dim(padded[2:4], (local_tile + offset) * TILE, 2 * TILE, 1)
        allowed = window_valid(tile_index, offset, padded_lengths, tile_count)
        tile_queries = queries[0]
        keyset = jnp.concatenate([span_part[0], cached[0]], 0)
        valueset = jnp.concatenate([span_part[1], cached[1]], 0)
        return attend(tile_queries, keyset, valueset, allowed)

    attended = jax.vmap(one_tile)(jnp.arange(tiles_here, dtype=jnp.int32)).reshape(
        tiles_here * TILE, queries.shape[2]
    )
    whole_weight = lax.all_gather(out_weight, ("seq", "fsdp"), axis=0, tiled=True)
    projected = jnp.dot(attended, whole_weight, preferred_element_type=jnp.float32)
    result = residual[0].astype(jnp.float32) + gate_scale[0][None, :] * projected
    return result.astype(jnp.bfloat16)[None]


def order(groups, stages, depth):
    count = max(groups, stages)
    steps = []
    for i in range(count):
        steps += [(act, i, 0) for act in "BD" if i < stages]
        steps += [("Q", i, 0)] * (i < groups)
    steps += [(act, k, 0) for act in "HP" for k in range(stages)]
    steps += [("T", g, 0) for g in range(groups)]
    steps += [("M", 0, 0)]
    for i in range(count):
        if i < stages and depth > 2:
            steps.append(("R", i, 1))
        if 1 <= i < groups:
            steps.append(("M", i, 0))
    for i in range(count):
        steps += [("F", i, 0)] * (i < groups)
        steps += [("R", i, hop) for hop in range(2, depth - 1) if i < stages]
    return steps


def kernel(
    n, groups, stages,
    off_ref, len_ref, q_hbm, kv_hbm, w_hbm, out_ref,
    qall, kv, bias, own_o, own_s, osend, orecv, abuf, wbuf, csend,
    load_sem, own_w_sem, own_c_sem,
    q_ss, q_rs, o_ss, o_rs, a_ss, a_rs, w_ss, w_rs, z_ss, z_rs, p_ss, p_rs, c_ss, c_rs,
    d_ss, d_rs, e_ss, e_rs,
):
    s = lax.axis_index("seq")
    x = lax.axis_index("fsdp")
    core = s % 2
    y = (s // 2) % 2
    z = s // 4
    depth = n // 4
    rows = w_hbm.shape[0]
    width = w_hbm.shape[1] // 4
    piece = width // stages
    per = HEADS // groups
    span = per * HDIM
    block = span + STATS
    me = y * 2 + x
    has_left, has_right = s > 0, s < n - 1
    has_down, has_up = z > 0, z < depth - 1

    def at(seq, fsdp):
        return {"seq": seq, "fsdp": fsdp}

    left, right = at(s - 1, x), at(s + 1, x)
    down, up = at(s - 4, x), at(s + 4, x)
    partner = at(s + 1 - 2 * core, x)
    s_y = s + 2 - 4 * y
    peers = (
        (at(s, 1 - x), y * 2 + 1 - x),
        (at(s_y, x), (1 - y) * 2 + x),
        (at(s_y, 1 - x), (1 - y) * 2 + 1 - x),
    )
    sides = ((has_left, left), (has_right, right))
    thin_out = ((z == depth - 2) & (y == 1), (z == 1) & (y == 0))
    thin_in = ((z == depth - 1) & (y == 1), (z == 0) & (y == 0))
    end_out = (z == depth - 2, z == 1)
    end_in = (z == depth - 1, z == 0)
    gives_up, gives_down = (z == depth - 2) & (y == 0), (z == 1) & (y == 1)
    gives = gives_up | gives_down
    takes = thin_in[0] | thin_in[1]
    over = jnp.where(gives_up, s + 6, s - 6)
    under = jnp.where(thin_in[0], s - 6, s + 6)
    across = (x, 1 - x)

    def remote(src, dst, ss, rs, to):
        return pltpu.make_async_remote_copy(
            src_ref=src, dst_ref=dst, send_sem=ss, recv_sem=rs, device_id=to, device_id_type=MESH
        )

    load_q = pltpu.make_async_copy(q_hbm.at[0], qall.at[pl.ds(TILE, TILE)], load_sem.at[0])
    load_kv = pltpu.make_async_copy(kv_hbm.at[0], kv, load_sem.at[1])
    load_kv.start()
    load_q.start()

    barrier = pltpu.get_barrier_semaphore()
    for to, _ in peers:
        pl.semaphore_signal(barrier, inc=1, device_id=to, device_id_type=MESH)
    for there, to in sides + ((has_down, down), (has_up, up)):
        @pl.when(there)
        def _(to=to):
            pl.semaphore_signal(barrier, inc=1, device_id=to, device_id_type=MESH)
    for there, seq in ((gives, over), (takes, under)):
        @pl.when(there)
        def _(seq=seq):
            for fsdp in across:
                pl.semaphore_signal(
                    barrier, inc=1, device_id=at(seq, fsdp), device_id_type=MESH
                )
    met = [there.astype(jnp.int32) for there in (has_left, has_right, has_down, has_up)]
    met += [2 * there.astype(jnp.int32) for there in (gives, takes)]
    pl.semaphore_wait(barrier, 3 + sum(met))

    def cols(g):
        return pl.ds(pl.multiple_of(g * span, span), span)

    def q_copy(side, g):
        to = sides[side][1]
        dst = qall.at[pl.ds((1 - side) * 2 * TILE, TILE), cols(g)]
        return remote(q_hbm.at[0, :, cols(g)], dst, q_ss.at[side, g], q_rs.at[1 - side, g], to)

    def q_arrival(side, g):
        dst = qall.at[pl.ds(side * 2 * TILE, TILE), cols(g)]
        return remote(dst, dst, q_ss.at[side, g], q_rs.at[side, g], sides[side][1])

    def part(g):
        return pl.ds(pl.multiple_of(g * block, 16), block)

    def o_copy(side, g):
        to = sides[side][1]
        return remote(
            osend.at[side, part(g)], orecv.at[1 - side, part(g)],
            o_ss.at[side, g], o_rs.at[1 - side, g], to,
        )

    def o_arrival(side, g):
        dst = orecv.at[side, part(g)]
        return remote(dst, dst, o_ss.at[side, g], o_rs.at[side, g], sides[side][1])

    def a_copy(kind, g):
        slot = peers[1][1] if kind == 2 else me
        block = abuf.at[pl.ds(pl.multiple_of(slot * TILE, TILE), TILE), cols(g)]
        to = peers[kind % 2][0]
        return remote(block, block, a_ss.at[kind, g], a_rs.at[kind, g], to)

    def a_arrival(kind, g):
        theirs = abuf.at[pl.ds(pl.multiple_of(peers[kind][1] * TILE, TILE), TILE), cols(g)]
        return remote(theirs, theirs, a_ss.at[kind, g], a_rs.at[kind, g], peers[kind][0])

    def w_piece(slot, k):
        return w_hbm.at[:, pl.ds(pl.multiple_of(slot * width + k * piece, piece), piece)]

    def w_slot(k, y_of, x_of):
        return wbuf.at[k, z, y_of, core, pl.ds(pl.multiple_of(x_of * rows, rows), rows)]

    def w_own(k):
        return pltpu.make_async_copy(w_piece(me, k), w_slot(k, y, x), own_w_sem.at[k])

    def w_copy(kind, k):
        to, slot = peers[kind]
        return remote(w_piece(slot, k), w_slot(k, y, x), w_ss.at[kind, k], w_rs.at[kind, k], to)

    def w_arrival(kind, k):
        to, slot = peers[kind]
        dst = w_slot(k, slot // 2, slot % 2)
        return remote(dst, dst, w_ss.at[kind, k], w_rs.at[kind, k], to)

    def d_copy(kind, k):
        slot = (1 - y) * 2 + across[kind]
        return remote(
            w_piece(slot, k), w_slot(k, y, x), d_ss.at[kind, k], d_rs.at[kind, k],
            at(over, across[kind]),
        )

    def d_arrival(kind, k):
        plane = jnp.where(thin_in[0], z - 1, z + 1)
        dst = wbuf.at[
            k, plane, 1 - y, core, pl.ds(pl.multiple_of(across[kind] * rows, rows), rows)
        ]
        return remote(dst, dst, d_ss.at[kind, k], d_rs.at[kind, k], at(under, across[kind]))

    def z_block(way, hop, k, half):
        plane = z - hop if way == 0 else z + hop
        return wbuf.at[k, plane, y, core] if half else wbuf.at[k, plane, :, core]

    def z_copy(way, hop, k, half):
        block = z_block(way, hop, k, half)
        return remote(
            block, block, z_ss.at[way, hop, k], z_rs.at[way, hop, k], up if way == 0 else down
        )

    def z_arrival(way, hop, k, half):
        block = z_block(way, hop, k, half)
        return remote(
            block, block, z_ss.at[way, hop - 1, k], z_rs.at[way, hop - 1, k],
            down if way == 0 else up,
        )

    def e_copy(way, k):
        block = wbuf.at[k, z, 1 - y, core]
        return remote(
            block, block, e_ss.at[way, k], e_rs.at[way, k], up if way == 0 else down
        )

    def e_arrival(way, k):
        block = wbuf.at[k, z - 1 if way == 0 else z + 1, 1 - y, core]
        return remote(
            block, block, e_ss.at[way, k], e_rs.at[way, k], down if way == 0 else up
        )

    def early(k, act):
        for way in range(2):
            @pl.when(end_out[way])
            def _(way=way):
                act(z_copy(way, 0, k, True))

    def late(k, act):
        for way, there in enumerate((has_up, has_down)):
            @pl.when(there & jnp.logical_not(end_out[way]))
            def _(way=way):
                act(z_copy(way, 0, k, False))

            @pl.when(end_out[way] & jnp.logical_not(thin_out[way]))
            def _(way=way):
                act(e_copy(way, k))

    def z_in(way, hop, k):
        if hop > 1:
            z_arrival(way, hop, k, False).wait_recv()
            return

        @pl.when(end_in[way])
        def _():
            z_arrival(way, hop, k, True).wait_recv()

        @pl.when(thin_in[way])
        def _():
            for kind in range(2):
                d_arrival(kind, k).wait_recv()

        @pl.when(end_in[way] & jnp.logical_not(thin_in[way]))
        def _():
            e_arrival(way, k).wait_recv()

        @pl.when(jnp.logical_not(end_in[way]))
        def _():
            z_arrival(way, hop, k, False).wait_recv()

    def p_copy(plane, k):
        block = wbuf.at[k, plane, :, core]
        return remote(block, block, p_ss.at[plane, k], p_rs.at[plane, k], partner)

    def p_arrival(plane, k):
        block = wbuf.at[k, plane, :, 1 - core]
        return remote(block, block, p_ss.at[plane, k], p_rs.at[plane, k], partner)

    def c_place(slot, k):
        return out_ref.at[:, pl.ds(pl.multiple_of(slot * width + k * piece, piece), piece)]

    def c_rows(slot, k):
        return csend.at[k, pl.ds(pl.multiple_of(slot * TILE, TILE), TILE)]

    def c_own(k):
        return pltpu.make_async_copy(c_rows(me, k), c_place(me, k), own_c_sem.at[k])

    def c_copy(kind, k):
        to, slot = peers[kind]
        return remote(c_rows(slot, k), c_place(me, k), c_ss.at[kind, k], c_rs.at[kind, k], to)

    def c_arrival(kind, k):
        to, slot = peers[kind]
        dst = c_place(slot, k)
        return remote(dst, dst, c_ss.at[kind, k], c_rs.at[kind, k], to)

    def each(count, body):
        lax.fori_loop(0, count, lambda i, c: (body(i), c)[1], jnp.int32(0))

    def on_sides(body):
        for side, (there, _) in enumerate(sides):
            @pl.when(there)
            def _(side=side):
                body(side)

    def relay(hop, k):
        for way, (there, onward) in enumerate(
            ((z >= hop, has_up), (z + hop < depth, has_down))
        ):
            @pl.when(there)
            def _(way=way, onward=onward):
                z_in(way, hop, k)
                if hop < depth - 1:
                    @pl.when(onward)
                    def _():
                        z_copy(way, hop, k, False).start()
                p_copy(z - hop if way == 0 else z + hop, k).start()

    def begin_w(k):
        w_own(k).start()
        for kind in range(3):
            w_copy(kind, k).start()

    def begin_d(k):
        @pl.when(gives)
        def _():
            for kind in range(2):
                d_copy(kind, k).start()

    def begin_q(g):
        on_sides(lambda side: q_copy(side, g).start())

    acts = {"B": begin_w, "D": begin_d, "Q": begin_q}
    steps = order(groups, stages, depth)
    first = [i for i, step in enumerate(steps) if step[0] not in acts][0]
    for act, which, _ in steps[:first]:
        acts[act](which)

    here = len_ref[0, s]
    for_left = jnp.where(off_ref[jnp.maximum(s - 1, 0)] == 1, here, 0)
    for_right = jnp.where(off_ref[jnp.minimum(s + 1, n - 1)] == 0, here, 0)
    lane = lax.broadcasted_iota(jnp.int32, (TILE, 3 * TILE), 1)
    row = lax.broadcasted_iota(jnp.int32, (TILE, 3 * TILE), 0)
    limit = jnp.where(lane < TILE, for_left, jnp.where(lane < 2 * TILE, here, for_right))
    bias[...] = jnp.where(row < limit, 0.0, NEG)

    for side, (there, _) in enumerate(sides):
        @pl.when(jnp.logical_not(there))
        def _(side=side):
            qall[pl.ds(side * 2 * TILE, TILE), :] = jnp.zeros((TILE, HEADS * HDIM), jnp.bfloat16)
            orecv[side] = jnp.zeros((groups * block, TILE), jnp.bfloat16)
            for g in range(groups):
                orecv[side, g * block + span : (g + 1) * block, :] = jnp.full(
                    (STATS, TILE), NEG, jnp.bfloat16
                )

    def own_rows(k):
        w_own(k).wait()
        w_arrival(0, k).wait_recv()
        early(k, lambda copy: copy.start())

    def plane_step(k):
        for kind in range(1, 3):
            w_arrival(kind, k).wait_recv()
        late(k, lambda copy: copy.start())
        p_copy(z, k).start()

    load_q.wait()
    load_kv.wait()

    def attend_group(g):
        on_sides(lambda side: q_arrival(side, g).wait_recv())

        def head(i):
            at_head = pl.ds(pl.multiple_of((g * per + i) * HDIM, HDIM), HDIM)
            keys = jnp.concatenate([kv[0, :, at_head], kv[2, :, at_head]], 0)
            values = jnp.concatenate([kv[1, :, at_head], kv[3, :, at_head]], 0)
            asked = qall[:, at_head]
            scores = lax.dot_general(
                keys, asked, (((1,), (1,)), ((), ())), preferred_element_type=jnp.float32
            )
            near = scores[:TILE]
            far = scores[TILE:] + bias[...]
            peak = jnp.maximum(
                jnp.max(near, axis=0, keepdims=True), jnp.max(far, axis=0, keepdims=True)
            )
            near = jnp.exp2((near - peak) * SCALE2)
            far = jnp.exp2((far - peak) * SCALE2)
            total = jnp.sum(near, axis=0, keepdims=True) + jnp.sum(far, axis=0, keepdims=True)
            weights = jnp.concatenate([near, far], 0).astype(jnp.bfloat16)
            mixed = lax.dot_general(
                values, weights, (((0,), (0,)), ((), ())), preferred_element_type=jnp.float32
            )
            mixed = mixed * (1.0 / total)
            level = peak * SCALE + jnp.log(total)
            there = pl.ds(g * block + i * HDIM, HDIM)
            osend[0, there, :] = mixed[:, :TILE].astype(jnp.bfloat16)
            own_o[at_head, :] = mixed[:, TILE : 2 * TILE]
            osend[1, there, :] = mixed[:, 2 * TILE :].astype(jnp.bfloat16)
            return level

        levels = jnp.concatenate([head(i) for i in range(per)], 0)
        own_s[g, :per, :] = levels[:, TILE : 2 * TILE]
        high = levels.astype(jnp.bfloat16)
        rest = levels - high.astype(jnp.float32)
        middle = rest.astype(jnp.bfloat16)
        low = (rest - middle.astype(jnp.float32)).astype(jnp.bfloat16)
        pad = jnp.zeros((STATS - 3 * per, 3 * TILE), jnp.float32)
        stats = jnp.concatenate([v.astype(jnp.float32) for v in (high, middle, low)] + [pad], 0)
        stats = stats.astype(jnp.bfloat16)
        at_stats = pl.ds(g * block + span, STATS)
        osend[0, at_stats, :] = stats[:, :TILE]
        osend[1, at_stats, :] = stats[:, 2 * TILE :]
        on_sides(lambda side: o_copy(side, g).start())

    def merge_group(g):
        on_sides(lambda side: o_arrival(side, g).wait_recv())

        def levels_of(side):
            stats = orecv[side, pl.ds(g * block + span, STATS), :].astype(jnp.float32)
            return stats[:per] + stats[per : 2 * per] + stats[2 * per : 3 * per]

        from_left, from_right = levels_of(0), levels_of(1)

        def head(i):
            at_head = pl.ds(pl.multiple_of((g * per + i) * HDIM, HDIM), HDIM)
            l0 = own_s[g, pl.ds(i, 1), :]
            l1 = from_left[i : i + 1]
            l2 = from_right[i : i + 1]
            there = pl.ds(g * block + i * HDIM, HDIM)
            top = jnp.maximum(l0, jnp.maximum(l1, l2))
            e0, e1, e2 = jnp.exp(l0 - top), jnp.exp(l1 - top), jnp.exp(l2 - top)
            both = e0 + e1 + e2
            part = 1.0 / both
            total = (
                own_o[at_head, :] * (e0 * part)
                + orecv[0, there, :].astype(jnp.float32) * (e1 * part)
                + orecv[1, there, :].astype(jnp.float32) * (e2 * part)
            )
            mine = pl.ds(pl.multiple_of(me * TILE, TILE), TILE)
            abuf[mine, at_head] = jnp.transpose(total.astype(jnp.bfloat16))

        for i in range(per):
            head(i)
        a_copy(1, g).start()
        a_copy(0, g).start()

    def forward(g):
        a_arrival(1, g).wait_recv()
        a_copy(2, g).start()

    acts |= {"H": own_rows, "P": plane_step, "T": attend_group, "M": merge_group, "F": forward}
    for act, which, hop in steps[first:]:
        if act == "R":
            relay(hop, which)
        else:
            acts[act](which)

    def a_wait(g):
        a_arrival(0, g).wait_recv()
        a_arrival(2, g).wait_recv()

    each(groups, a_wait)

    def stage(k):
        if depth > 1:
            relay(depth - 1, k)
        for plane in range(depth):
            p_arrival(plane, k).wait_recv()
        block = wbuf[k].reshape(n * 2 * rows, piece)
        product = jnp.dot(abuf[...], block, preferred_element_type=jnp.float32)
        csend[k] = product.astype(jnp.bfloat16)
        for kind in range(3):
            c_copy(kind, k).start()
        c_own(k).start()

    each(stages, stage)

    def finish_stage(k):
        c_own(k).wait()
        for kind in range(3):
            c_copy(kind, k).wait_send()
            c_arrival(kind, k).wait_recv()

    def finish_weights(k):
        for kind in range(3):
            w_copy(kind, k).wait_send()

        @pl.when(gives)
        def _():
            for kind in range(2):
                d_copy(kind, k).wait_send()

        for plane in range(depth):
            p_copy(plane, k).wait_send()
        early(k, lambda copy: copy.wait_send())
        late(k, lambda copy: copy.wait_send())
        for hop in range(1, depth - 1):
            for way, there in enumerate(
                (has_up & (z >= hop), has_down & (z + hop < depth))
            ):
                @pl.when(there)
                def _(way=way, hop=hop):
                    z_copy(way, hop, k, False).wait_send()

    def finish_group(g):
        for kind in range(3):
            a_copy(kind, g).wait_send()

        def sent(side):
            q_copy(side, g).wait_send()
            o_copy(side, g).wait_send()

        on_sides(sent)

    each(groups, finish_group)
    each(stages, finish_weights)
    each(stages, finish_stage)


GROUPS = 5
STATS = 16
PIECE = 256


def fused(queries, key_value_sets, cache_offsets, cache_lengths, out_weight, residual, gate_scale):
    n = lax.axis_size("seq")
    inner = queries.shape[2]
    rows, model = out_weight.shape
    depth = n // 4
    stages = model // 4 // PIECE
    bf16, f32 = jnp.bfloat16, jnp.float32
    dma = pltpu.SemaphoreType.DMA
    smem = pl.BlockSpec(memory_space=pltpu.SMEM)
    hbm = pl.BlockSpec(memory_space=pltpu.HBM)
    projected = pl.pallas_call(
        functools.partial(kernel, n, GROUPS, stages),
        out_shape=jax.ShapeDtypeStruct((TILE, model), bf16),
        in_specs=[smem, smem, hbm, hbm, hbm],
        out_specs=pl.BlockSpec(memory_space=pl.ANY),
        scratch_shapes=[
            pltpu.VMEM((3 * TILE, inner), bf16),
            pltpu.VMEM((4, TILE, inner), bf16),
            pltpu.VMEM((TILE, 3 * TILE), f32),
            pltpu.VMEM((inner, TILE), f32),
            pltpu.VMEM((GROUPS, 8, TILE), f32),
            pltpu.VMEM((2, inner + GROUPS * STATS, TILE), bf16),
            pltpu.VMEM((2, inner + GROUPS * STATS, TILE), bf16),
            pltpu.VMEM((4 * TILE, inner), bf16),
            pltpu.VMEM((stages, depth, 2, 2, 2 * rows, PIECE), bf16),
            pltpu.VMEM((stages, 4 * TILE, PIECE), bf16),
            dma((2,)), dma((stages,)), dma((stages,)),
            dma((2, GROUPS)), dma((2, GROUPS)),
            dma((2, GROUPS)), dma((2, GROUPS)),
            dma((3, GROUPS)), dma((3, GROUPS)),
            dma((3, stages)), dma((3, stages)),
            dma((2, depth, stages)), dma((2, depth, stages)),
            dma((depth, stages)), dma((depth, stages)),
            dma((3, stages)), dma((3, stages)),
            dma((2, stages)), dma((2, stages)),
            dma((2, stages)), dma((2, stages)),
        ],
        compiler_params=pltpu.CompilerParams(
            collective_id=0, has_side_effects=True, vmem_limit_bytes=56 * 2**20
        ),
    )(cache_offsets, cache_lengths, queries, key_value_sets, out_weight)
    result = residual[0].astype(f32) + gate_scale[0][None, :] * projected.astype(f32)
    return result.astype(bf16)[None]


def shards(queries, key_value_sets, cache_offsets, cache_lengths, out_weight, residual, gate_scale):
    args = (
        queries, key_value_sets, cache_offsets, cache_lengths, out_weight, residual, gate_scale
    )
    n, f = lax.axis_size("seq"), lax.axis_size("fsdp")
    rows, model = out_weight.shape
    suits = (
        f == 2
        and n % 4 == 0
        and n > 4
        and queries.shape[:2] == (1, TILE)
        and cache_lengths.shape[1] == n
        and rows % 16 == 0
        and model % (4 * PIECE) == 0
        and HEADS % GROUPS == 0
        and 3 * (HEADS // GROUPS) <= STATS
    )
    return fused(*args) if suits else plain(*args)


def solution(mesh):
    placed = (
        P("fsdp", "seq", None),
        P("fsdp", None, "seq", None),
        P(),
        P("fsdp", None),
        P(("seq", "fsdp"), None),
        P("fsdp", "seq", None),
        P("fsdp", None),
    )
    return jax.shard_map(
        shards, mesh=mesh, in_specs=placed, out_specs=P("fsdp", "seq", None), check_vma=False
    )
```

```python
import functools
import math

import jax
import jax.numpy as jnp
from jax import lax
from jax.experimental import pallas as pl
from jax.experimental.pallas import tpu as pltpu
from jax.sharding import PartitionSpec as P

HDIM = 128
HEADS = 20
TILE = 128
NEG = -1e30
SCALE = 1.0 / math.sqrt(HDIM)
SCALE2 = SCALE / math.log(2.0)
MESH = pl.DeviceIdType.MESH


def extended(cells, sides, width):
    for axis, dim in sides:
        count = lax.axis_size(axis)
        ends = count - 1
        head = lax.slice_in_dim(cells, 0, width, axis=dim)
        tail = lax.slice_in_dim(cells, cells.shape[dim] - width, cells.shape[dim], axis=dim)
        cells = jnp.concatenate(
            [
                lax.ppermute(tail, axis, [(i, (i + 1) % count) for i in range(ends)]),
                cells,
                lax.ppermute(head, axis, [((i + 1) % count, i) for i in range(ends)]),
            ],
            axis=dim,
        )
    return cells


def window_valid(tile_index, offset, padded_lengths, tile_count):
    span_tiles = tile_index - 1 + jnp.arange(3, dtype=jnp.int32)
    span_allowed = jnp.repeat((span_tiles >= 0) & (span_tiles < tile_count), TILE)
    first_cache = tile_index - 1 + offset
    cache_counts = lax.dynamic_slice_in_dim(padded_lengths, first_cache + 1, 2)
    positions = jnp.arange(TILE, dtype=jnp.int32)
    cache_allowed = (positions[None, :] < cache_counts[:, None]).reshape(2 * TILE)
    return jnp.concatenate([span_allowed, cache_allowed])


def attend(tile_queries, keyset, valueset, allowed):
    query_heads = tile_queries.reshape(TILE, HEADS, HDIM)
    key_heads = keyset.reshape(5 * TILE, HEADS, HDIM)
    value_heads = valueset.reshape(5 * TILE, HEADS, HDIM)
    scores = (
        jnp.einsum("qhd,khd->hqk", query_heads, key_heads, preferred_element_type=jnp.float32)
        * SCALE
    )
    scores = jnp.where(allowed[None, None, :], scores, NEG)
    row_peak = jnp.max(scores, axis=-1, keepdims=True)
    expont = jnp.exp(scores - row_peak)
    probs = (expont / jnp.sum(expont, axis=-1, keepdims=True)).astype(jnp.bfloat16)
    attended = jnp.einsum("hqk,khd->qhd", probs, value_heads, preferred_element_type=jnp.float32)
    return attended.reshape(TILE, HEADS * HDIM).astype(jnp.bfloat16)


def plain(queries, key_value_sets, cache_offsets, cache_lengths, out_weight, residual, gate_scale):
    tile_count = cache_lengths.shape[1]
    tiles_here = queries.shape[1] // TILE
    device = lax.axis_index("seq")
    padded = extended(key_value_sets, (("seq", 2),), TILE)[0]
    padded_lengths = jnp.pad(cache_lengths[0], 1)

    def one_tile(local_tile):
        tile_index = device * tiles_here + local_tile
        span_part = padded[0:2]
        offset = cache_offsets[tile_index]
        cached = lax.dynamic_slice_in_dim(padded[2:4], (local_tile + offset) * TILE, 2 * TILE, 1)
        allowed = window_valid(tile_index, offset, padded_lengths, tile_count)
        tile_queries = queries[0]
        keyset = jnp.concatenate([span_part[0], cached[0]], 0)
        valueset = jnp.concatenate([span_part[1], cached[1]], 0)
        return attend(tile_queries, keyset, valueset, allowed)

    attended = jax.vmap(one_tile)(jnp.arange(tiles_here, dtype=jnp.int32)).reshape(
        tiles_here * TILE, queries.shape[2]
    )
    whole_weight = lax.all_gather(out_weight, ("seq", "fsdp"), axis=0, tiled=True)
    projected = jnp.dot(attended, whole_weight, preferred_element_type=jnp.float32)
    result = residual[0].astype(jnp.float32) + gate_scale[0][None, :] * projected
    return result.astype(jnp.bfloat16)[None]


def order(groups, stages, depth):
    count = max(groups, stages)
    steps = []
    for i in range(count):
        steps += [(act, i, 0) for act in "BD" if i < stages]
        steps += [("Q", i, 0)] * (i < groups)
    steps += [(act, k, 0) for act in "HP" for k in range(stages)]
    steps += [("T", g, 0) for g in range(groups)]
    steps += [("M", 0, 0)]
    for i in range(count):
        if i < stages and depth > 2:
            steps.append(("R", i, 1))
        if 1 <= i < groups:
            steps.append(("M", i, 0))
    for i in range(count):
        steps += [("F", i, 0)] * (i < groups)
        steps += [("R", i, hop) for hop in range(2, depth - 1) if i < stages]
    return steps


def kernel(
    n, groups, stages,
    off_ref, len_ref, q_hbm, kv_hbm, w_hbm, out_ref,
    qall, kv, bias, own_o, own_s, osend, orecv, abuf, wbuf, csend,
    load_sem, own_w_sem, own_c_sem,
    q_ss, q_rs, o_ss, o_rs, a_ss, a_rs, w_ss, w_rs, z_ss, z_rs, p_ss, p_rs, c_ss, c_rs,
    d_ss, d_rs, e_ss, e_rs,
):
    s = lax.axis_index("seq")
    x = lax.axis_index("fsdp")
    core = s % 2
    y = (s // 2) % 2
    z = s // 4
    depth = n // 4
    rows = w_hbm.shape[0]
    width = w_hbm.shape[1] // 4
    piece = width // stages
    per = HEADS // groups
    span = per * HDIM
    block = span + STATS
    me = y * 2 + x
    has_left, has_right = s > 0, s < n - 1
    has_down, has_up = z > 0, z < depth - 1

    def at(seq, fsdp):
        return {"seq": seq, "fsdp": fsdp}

    left, right = at(s - 1, x), at(s + 1, x)
    down, up = at(s - 4, x), at(s + 4, x)
    partner = at(s + 1 - 2 * core, x)
    s_y = s + 2 - 4 * y
    peers = (
        (at(s, 1 - x), y * 2 + 1 - x),
        (at(s_y, x), (1 - y) * 2 + x),
        (at(s_y, 1 - x), (1 - y) * 2 + 1 - x),
    )
    sides = ((has_left, left), (has_right, right))
    thin_out = ((z == depth - 2) & (y == 1), (z == 1) & (y == 0))
    thin_in = ((z == depth - 1) & (y == 1), (z == 0) & (y == 0))
    end_out = (z == depth - 2, z == 1)
    end_in = (z == depth - 1, z == 0)
    gives_up, gives_down = (z == depth - 2) & (y == 0), (z == 1) & (y == 1)
    gives = gives_up | gives_down
    takes = thin_in[0] | thin_in[1]
    over = jnp.where(gives_up, s + 6, s - 6)
    under = jnp.where(thin_in[0], s - 6, s + 6)
    across = (x, 1 - x)

    def remote(src, dst, ss, rs, to):
        return pltpu.make_async_remote_copy(
            src_ref=src, dst_ref=dst, send_sem=ss, recv_sem=rs, device_id=to, device_id_type=MESH
        )

    load_q = pltpu.make_async_copy(q_hbm.at[0], qall.at[pl.ds(TILE, TILE)], load_sem.at[0])
    load_kv = pltpu.make_async_copy(kv_hbm.at[0], kv, load_sem.at[1])

    barrier = pltpu.get_barrier_semaphore()
    for to, _ in peers:
        pl.semaphore_signal(barrier, inc=1, device_id=to, device_id_type=MESH)
    for there, to in sides + ((has_down, down), (has_up, up)):
        @pl.when(there)
        def _(to=to):
            pl.semaphore_signal(barrier, inc=1, device_id=to, device_id_type=MESH)
    for there, seq in ((gives, over), (takes, under)):
        @pl.when(there)
        def _(seq=seq):
            for fsdp in across:
                pl.semaphore_signal(
                    barrier, inc=1, device_id=at(seq, fsdp), device_id_type=MESH
                )
    met = [there.astype(jnp.int32) for there in (has_left, has_right, has_down, has_up)]
    met += [2 * there.astype(jnp.int32) for there in (gives, takes)]

    def cols(g):
        return pl.ds(pl.multiple_of(g * span, span), span)

    def q_copy(side, g):
        to = sides[side][1]
        dst = qall.at[pl.ds((1 - side) * 2 * TILE, TILE), cols(g)]
        return remote(q_hbm.at[0, :, cols(g)], dst, q_ss.at[side, g], q_rs.at[1 - side, g], to)

    def q_arrival(side, g):
        dst = qall.at[pl.ds(side * 2 * TILE, TILE), cols(g)]
        return remote(dst, dst, q_ss.at[side, g], q_rs.at[side, g], sides[side][1])

    def part(g):
        return pl.ds(pl.multiple_of(g * block, 16), block)

    def o_copy(side, g):
        to = sides[side][1]
        return remote(
            osend.at[side, part(g)], orecv.at[1 - side, part(g)],
            o_ss.at[side, g], o_rs.at[1 - side, g], to,
        )

    def o_arrival(side, g):
        dst = orecv.at[side, part(g)]
        return remote(dst, dst, o_ss.at[side, g], o_rs.at[side, g], sides[side][1])

    def a_copy(kind, g):
        slot = peers[1][1] if kind == 2 else me
        block = abuf.at[pl.ds(pl.multiple_of(slot * TILE, TILE), TILE), cols(g)]
        to = peers[kind % 2][0]
        return remote(block, block, a_ss.at[kind, g], a_rs.at[kind, g], to)

    def a_arrival(kind, g):
        theirs = abuf.at[pl.ds(pl.multiple_of(peers[kind][1] * TILE, TILE), TILE), cols(g)]
        return remote(theirs, theirs, a_ss.at[kind, g], a_rs.at[kind, g], peers[kind][0])

    def w_piece(slot, k):
        return w_hbm.at[:, pl.ds(pl.multiple_of(slot * width + k * piece, piece), piece)]

    def w_slot(k, y_of, x_of):
        return wbuf.at[k, z, y_of, core, pl.ds(pl.multiple_of(x_of * rows, rows), rows)]

    def w_own(k):
        return pltpu.make_async_copy(w_piece(me, k), w_slot(k, y, x), own_w_sem.at[k])

    def w_copy(kind, k):
        to, slot = peers[kind]
        return remote(w_piece(slot, k), w_slot(k, y, x), w_ss.at[kind, k], w_rs.at[kind, k], to)

    def w_arrival(kind, k):
        to, slot = peers[kind]
        dst = w_slot(k, slot // 2, slot % 2)
        return remote(dst, dst, w_ss.at[kind, k], w_rs.at[kind, k], to)

    def d_copy(kind, k):
        slot = (1 - y) * 2 + across[kind]
        return remote(
            w_piece(slot, k), w_slot(k, y, x), d_ss.at[kind, k], d_rs.at[kind, k],
            at(over, across[kind]),
        )

    def d_arrival(kind, k):
        plane = jnp.where(thin_in[0], z - 1, z + 1)
        dst = wbuf.at[
            k, plane, 1 - y, core, pl.ds(pl.multiple_of(across[kind] * rows, rows), rows)
        ]
        return remote(dst, dst, d_ss.at[kind, k], d_rs.at[kind, k], at(under, across[kind]))

    def z_block(way, hop, k, half):
        plane = z - hop if way == 0 else z + hop
        return wbuf.at[k, plane, y, core] if half else wbuf.at[k, plane, :, core]

    def z_copy(way, hop, k, half):
        block = z_block(way, hop, k, half)
        return remote(
            block, block, z_ss.at[way, hop, k], z_rs.at[way, hop, k], up if way == 0 else down
        )

    def z_arrival(way, hop, k, half):
        block = z_block(way, hop, k, half)
        return remote(
            block, block, z_ss.at[way, hop - 1, k], z_rs.at[way, hop - 1, k],
            down if way == 0 else up,
        )

    def e_copy(way, k):
        block = wbuf.at[k, z, 1 - y, core]
        return remote(
            block, block, e_ss.at[way, k], e_rs.at[way, k], up if way == 0 else down
        )

    def e_arrival(way, k):
        block = wbuf.at[k, z - 1 if way == 0 else z + 1, 1 - y, core]
        return remote(
            block, block, e_ss.at[way, k], e_rs.at[way, k], down if way == 0 else up
        )

    def early(k, act):
        for way in range(2):
            @pl.when(end_out[way])
            def _(way=way):
                act(z_copy(way, 0, k, True))

    def late(k, act):
        for way, there in enumerate((has_up, has_down)):
            @pl.when(there & jnp.logical_not(end_out[way]))
            def _(way=way):
                act(z_copy(way, 0, k, False))

            @pl.when(end_out[way] & jnp.logical_not(thin_out[way]))
            def _(way=way):
                act(e_copy(way, k))

    def z_in(way, hop, k):
        if hop > 1:
            z_arrival(way, hop, k, False).wait_recv()
            return

        @pl.when(end_in[way])
        def _():
            z_arrival(way, hop, k, True).wait_recv()

        @pl.when(thin_in[way])
        def _():
            for kind in range(2):
                d_arrival(kind, k).wait_recv()

        @pl.when(end_in[way] & jnp.logical_not(thin_in[way]))
        def _():
            e_arrival(way, k).wait_recv()

        @pl.when(jnp.logical_not(end_in[way]))
        def _():
            z_arrival(way, hop, k, False).wait_recv()

    def p_copy(plane, k):
        block = wbuf.at[k, plane, :, core]
        return remote(block, block, p_ss.at[plane, k], p_rs.at[plane, k], partner)

    def p_arrival(plane, k):
        block = wbuf.at[k, plane, :, 1 - core]
        return remote(block, block, p_ss.at[plane, k], p_rs.at[plane, k], partner)

    def c_place(slot, k):
        return out_ref.at[:, pl.ds(pl.multiple_of(slot * width + k * piece, piece), piece)]

    def c_rows(slot, k):
        return csend.at[k, pl.ds(pl.multiple_of(slot * TILE, TILE), TILE)]

    def c_own(k):
        return pltpu.make_async_copy(c_rows(me, k), c_place(me, k), own_c_sem.at[k])

    def c_copy(kind, k):
        to, slot = peers[kind]
        return remote(c_rows(slot, k), c_place(me, k), c_ss.at[kind, k], c_rs.at[kind, k], to)

    def c_arrival(kind, k):
        to, slot = peers[kind]
        dst = c_place(slot, k)
        return remote(dst, dst, c_ss.at[kind, k], c_rs.at[kind, k], to)

    def each(count, body):
        lax.fori_loop(0, count, lambda i, c: (body(i), c)[1], jnp.int32(0))

    def on_sides(body):
        for side, (there, _) in enumerate(sides):
            @pl.when(there)
            def _(side=side):
                body(side)

    def relay(hop, k):
        for way, (there, onward) in enumerate(
            ((z >= hop, has_up), (z + hop < depth, has_down))
        ):
            @pl.when(there)
            def _(way=way, onward=onward):
                z_in(way, hop, k)
                if hop < depth - 1:
                    @pl.when(onward)
                    def _():
                        z_copy(way, hop, k, False).start()
                p_copy(z - hop if way == 0 else z + hop, k).start()

    def begin_w(k):
        for kind in range(3):
            w_copy(kind, k).start()

    def begin_d(k):
        @pl.when(gives)
        def _():
            for kind in range(2):
                d_copy(kind, k).start()

    def begin_q(g):
        on_sides(lambda side: q_copy(side, g).start())

    for k in range(stages):
        w_own(k).start()
    pl.semaphore_wait(barrier, 3 + sum(met))

    acts = {"B": begin_w, "D": begin_d, "Q": begin_q}
    steps = order(groups, stages, depth)
    first = [i for i, step in enumerate(steps) if step[0] not in acts][0]
    for act, which, _ in steps[:first]:
        acts[act](which)

    load_kv.start()
    load_q.start()
    here = len_ref[0, s]
    for_left = jnp.where(off_ref[jnp.maximum(s - 1, 0)] == 1, here, 0)
    for_right = jnp.where(off_ref[jnp.minimum(s + 1, n - 1)] == 0, here, 0)
    lane = lax.broadcasted_iota(jnp.int32, (TILE, 3 * TILE), 1)
    row = lax.broadcasted_iota(jnp.int32, (TILE, 3 * TILE), 0)
    limit = jnp.where(lane < TILE, for_left, jnp.where(lane < 2 * TILE, here, for_right))
    bias[...] = jnp.where(row < limit, 0.0, NEG)

    for side, (there, _) in enumerate(sides):
        @pl.when(jnp.logical_not(there))
        def _(side=side):
            qall[pl.ds(side * 2 * TILE, TILE), :] = jnp.zeros((TILE, HEADS * HDIM), jnp.bfloat16)
            orecv[side] = jnp.zeros((groups * block, TILE), jnp.bfloat16)
            for g in range(groups):
                orecv[side, g * block + span : (g + 1) * block, :] = jnp.full(
                    (STATS, TILE), NEG, jnp.bfloat16
                )

    def own_rows(k):
        w_own(k).wait()
        w_arrival(0, k).wait_recv()
        early(k, lambda copy: copy.start())

    def plane_step(k):
        for kind in range(1, 3):
            w_arrival(kind, k).wait_recv()
        late(k, lambda copy: copy.start())
        p_copy(z, k).start()

    load_q.wait()
    load_kv.wait()

    def attend_group(g):
        on_sides(lambda side: q_arrival(side, g).wait_recv())

        def head(i):
            at_head = pl.ds(pl.multiple_of((g * per + i) * HDIM, HDIM), HDIM)
            keys = jnp.concatenate([kv[0, :, at_head], kv[2, :, at_head]], 0)
            values = jnp.concatenate([kv[1, :, at_head], kv[3, :, at_head]], 0)
            asked = qall[:, at_head]
            scores = lax.dot_general(
                keys, asked, (((1,), (1,)), ((), ())), preferred_element_type=jnp.float32
            )
            near = scores[:TILE]
            far = scores[TILE:] + bias[...]
            peak = jnp.maximum(
                jnp.max(near, axis=0, keepdims=True), jnp.max(far, axis=0, keepdims=True)
            )
            near = jnp.exp2((near - peak) * SCALE2)
            far = jnp.exp2((far - peak) * SCALE2)
            total = jnp.sum(near, axis=0, keepdims=True) + jnp.sum(far, axis=0, keepdims=True)
            weights = jnp.concatenate([near, far], 0).astype(jnp.bfloat16)
            mixed = lax.dot_general(
                values, weights, (((0,), (0,)), ((), ())), preferred_element_type=jnp.float32
            )
            mixed = mixed * (1.0 / total)
            level = peak * SCALE + jnp.log(total)
            there = pl.ds(g * block + i * HDIM, HDIM)
            osend[0, there, :] = mixed[:, :TILE].astype(jnp.bfloat16)
            own_o[at_head, :] = mixed[:, TILE : 2 * TILE]
            osend[1, there, :] = mixed[:, 2 * TILE :].astype(jnp.bfloat16)
            return level

        levels = jnp.concatenate([head(i) for i in range(per)], 0)
        own_s[g, :per, :] = levels[:, TILE : 2 * TILE]
        high = levels.astype(jnp.bfloat16)
        rest = levels - high.astype(jnp.float32)
        middle = rest.astype(jnp.bfloat16)
        low = (rest - middle.astype(jnp.float32)).astype(jnp.bfloat16)
        pad = jnp.zeros((STATS - 3 * per, 3 * TILE), jnp.float32)
        stats = jnp.concatenate([v.astype(jnp.float32) for v in (high, middle, low)] + [pad], 0)
        stats = stats.astype(jnp.bfloat16)
        at_stats = pl.ds(g * block + span, STATS)
        osend[0, at_stats, :] = stats[:, :TILE]
        osend[1, at_stats, :] = stats[:, 2 * TILE :]
        on_sides(lambda side: o_copy(side, g).start())

    def merge_group(g):
        on_sides(lambda side: o_arrival(side, g).wait_recv())

        def levels_of(side):
            stats = orecv[side, pl.ds(g * block + span, STATS), :].astype(jnp.float32)
            return stats[:per] + stats[per : 2 * per] + stats[2 * per : 3 * per]

        from_left, from_right = levels_of(0), levels_of(1)

        def head(i):
            at_head = pl.ds(pl.multiple_of((g * per + i) * HDIM, HDIM), HDIM)
            l0 = own_s[g, pl.ds(i, 1), :]
            l1 = from_left[i : i + 1]
            l2 = from_right[i : i + 1]
            there = pl.ds(g * block + i * HDIM, HDIM)
            top = jnp.maximum(l0, jnp.maximum(l1, l2))
            e0, e1, e2 = jnp.exp(l0 - top), jnp.exp(l1 - top), jnp.exp(l2 - top)
            both = e0 + e1 + e2
            part = 1.0 / both
            total = (
                own_o[at_head, :] * (e0 * part)
                + orecv[0, there, :].astype(jnp.float32) * (e1 * part)
                + orecv[1, there, :].astype(jnp.float32) * (e2 * part)
            )
            mine = pl.ds(pl.multiple_of(me * TILE, TILE), TILE)
            abuf[mine, at_head] = jnp.transpose(total.astype(jnp.bfloat16))

        for i in range(per):
            head(i)
        a_copy(1, g).start()
        a_copy(0, g).start()

    def forward(g):
        a_arrival(1, g).wait_recv()
        a_copy(2, g).start()

    acts |= {"H": own_rows, "P": plane_step, "T": attend_group, "M": merge_group, "F": forward}
    for act, which, hop in steps[first:]:
        if act == "R":
            relay(hop, which)
        else:
            acts[act](which)

    def a_wait(g):
        a_arrival(0, g).wait_recv()
        a_arrival(2, g).wait_recv()

    each(groups, a_wait)

    def stage(k):
        if depth > 1:
            relay(depth - 1, k)
        for plane in range(depth):
            p_arrival(plane, k).wait_recv()
        block = wbuf[k].reshape(n * 2 * rows, piece)
        product = jnp.dot(abuf[...], block, preferred_element_type=jnp.float32)
        csend[k] = product.astype(jnp.bfloat16)
        for kind in range(3):
            c_copy(kind, k).start()
        c_own(k).start()

    each(stages, stage)

    def finish_stage(k):
        c_own(k).wait()
        for kind in range(3):
            c_copy(kind, k).wait_send()
            c_arrival(kind, k).wait_recv()

    def finish_weights(k):
        for kind in range(3):
            w_copy(kind, k).wait_send()

        @pl.when(gives)
        def _():
            for kind in range(2):
                d_copy(kind, k).wait_send()

        for plane in range(depth):
            p_copy(plane, k).wait_send()
        early(k, lambda copy: copy.wait_send())
        late(k, lambda copy: copy.wait_send())
        for hop in range(1, depth - 1):
            for way, there in enumerate(
                (has_up & (z >= hop), has_down & (z + hop < depth))
            ):
                @pl.when(there)
                def _(way=way, hop=hop):
                    z_copy(way, hop, k, False).wait_send()

    def finish_group(g):
        for kind in range(3):
            a_copy(kind, g).wait_send()

        def sent(side):
            q_copy(side, g).wait_send()
            o_copy(side, g).wait_send()

        on_sides(sent)

    each(groups, finish_group)
    each(stages, finish_weights)
    each(stages, finish_stage)


GROUPS = 5
STATS = 16
PIECE = 256


def fused(queries, key_value_sets, cache_offsets, cache_lengths, out_weight, residual, gate_scale):
    n = lax.axis_size("seq")
    inner = queries.shape[2]
    rows, model = out_weight.shape
    depth = n // 4
    stages = model // 4 // PIECE
    bf16, f32 = jnp.bfloat16, jnp.float32
    dma = pltpu.SemaphoreType.DMA
    smem = pl.BlockSpec(memory_space=pltpu.SMEM)
    hbm = pl.BlockSpec(memory_space=pltpu.HBM)
    projected = pl.pallas_call(
        functools.partial(kernel, n, GROUPS, stages),
        out_shape=jax.ShapeDtypeStruct((TILE, model), bf16),
        in_specs=[smem, smem, hbm, hbm, hbm],
        out_specs=pl.BlockSpec(memory_space=pl.ANY),
        scratch_shapes=[
            pltpu.VMEM((3 * TILE, inner), bf16),
            pltpu.VMEM((4, TILE, inner), bf16),
            pltpu.VMEM((TILE, 3 * TILE), f32),
            pltpu.VMEM((inner, TILE), f32),
            pltpu.VMEM((GROUPS, 8, TILE), f32),
            pltpu.VMEM((2, inner + GROUPS * STATS, TILE), bf16),
            pltpu.VMEM((2, inner + GROUPS * STATS, TILE), bf16),
            pltpu.VMEM((4 * TILE, inner), bf16),
            pltpu.VMEM((stages, depth, 2, 2, 2 * rows, PIECE), bf16),
            pltpu.VMEM((stages, 4 * TILE, PIECE), bf16),
            dma((2,)), dma((stages,)), dma((stages,)),
            dma((2, GROUPS)), dma((2, GROUPS)),
            dma((2, GROUPS)), dma((2, GROUPS)),
            dma((3, GROUPS)), dma((3, GROUPS)),
            dma((3, stages)), dma((3, stages)),
            dma((2, depth, stages)), dma((2, depth, stages)),
            dma((depth, stages)), dma((depth, stages)),
            dma((3, stages)), dma((3, stages)),
            dma((2, stages)), dma((2, stages)),
            dma((2, stages)), dma((2, stages)),
        ],
        compiler_params=pltpu.CompilerParams(
            collective_id=0, has_side_effects=True, vmem_limit_bytes=56 * 2**20
        ),
    )(cache_offsets, cache_lengths, queries, key_value_sets, out_weight)
    result = residual[0].astype(f32) + gate_scale[0][None, :] * projected.astype(f32)
    return result.astype(bf16)[None]


def shards(queries, key_value_sets, cache_offsets, cache_lengths, out_weight, residual, gate_scale):
    args = (
        queries, key_value_sets, cache_offsets, cache_lengths, out_weight, residual, gate_scale
    )
    n, f = lax.axis_size("seq"), lax.axis_size("fsdp")
    rows, model = out_weight.shape
    suits = (
        f == 2
        and n % 4 == 0
        and n > 4
        and queries.shape[:2] == (1, TILE)
        and cache_lengths.shape[1] == n
        and rows % 16 == 0
        and model % (4 * PIECE) == 0
        and HEADS % GROUPS == 0
        and 3 * (HEADS // GROUPS) <= STATS
    )
    return fused(*args) if suits else plain(*args)


def solution(mesh):
    placed = (
        P("fsdp", "seq", None),
        P("fsdp", None, "seq", None),
        P(),
        P("fsdp", None),
        P(("seq", "fsdp"), None),
        P("fsdp", "seq", None),
        P("fsdp", None),
    )
    return jax.shard_map(
        shards, mesh=mesh, in_specs=placed, out_specs=P("fsdp", "seq", None), check_vma=False
    )
```
